32 devices in a mesh: groups: 2 (over y), row: 2 (over x), col: 4 (over z), dp: 2 (over core).
Axes of the slice: x: 2, y: 2, z: 4, core: 2. Of those that a mesh axis runs over, the one named last changes fastest.
Arguments:
- features: bfloat16 [4, 512, 6144], P(('groups', 'dp'), 'row', 'col'), parts along dimension 0, may hold values from -6 to 6
- output_gradient: bfloat16 [4, 512, 6144], P(('groups', 'dp'), 'row', 'col'), parts along dimension 0, may hold values from -6 to 6
- value_weight: bfloat16 [6144, 6144], P('row', 'col'), may hold values from -0.109375 to 0.109375
- gate_weight: bfloat16 [6144, 6144], P('row', 'col'), may hold values from -1 to 1
- mixer_weight: bfloat16 [6144, 6144], P('row', 'col'), may hold values from -0.109375 to 0.109375
- conv_kernel: float32 [31, 6144], P(None, 'col'), may hold values from -1 to 1
- layer_norm_gain: float32 [6144], replicated, may hold values from 0.3 to 4.2
Outputs:
- module_out: bfloat16 [4, 512, 6144], P(('groups', 'dp'), 'row', 'col'), parts along dimension 0
- input_gradient: bfloat16 [4, 512, 6144], P(('groups', 'dp'), 'row', 'col'), parts along dimension 0
- value_weight_grad: float32 [12288, 6144], P(('groups', 'row', 'dp'), 'col'), parts along dimension 0
- gate_weight_grad: float32 [12288, 6144], P(('groups', 'row', 'dp'), 'col'), parts along dimension 0
- mixer_weight_grad: float32 [12288, 6144], P(('groups', 'row', 'dp'), 'col'), parts along dimension 0
- kernel_grad: float32 [62, 6144], P('groups', 'col'), parts along dimension 0
- norm_gain_gradient: float32 [12288], P(('groups', 'col')), parts along dimension 0
The draws below stay inside these ranges and needn't reach their ends.
There are 2 independent parts, one for each index of `groups`. The reference program is written for one: setup_inputs(seed, part) draws one part's arguments, and reference() takes and returns one part's arrays. A program takes and returns all parts, laid end to end along the dimension named above; an argument that names none is the same for every part. Nothing has to cross between parts.
All inputs are finite; a program needn't handle non-finite values.
Results may differ from the reference program's by a relative error of at most 0.02.
Values may be sent and summed in bfloat16 or wider, within the bound.
A program may use at most 320 MiB of HBM per device.

```python
import math
import jax
import jax.numpy as jnp
from jax import lax

MODEL_WIDTH = 6144
KERNEL = 31
TF_DEV = 256
UTT_DEV = 1
FRAMES = 512
UTT = 2
N_ROW = 2
N_COL = 4
N_DP = 2


def draw_layer_norm_gain(key, part):
    position = jnp.arange(MODEL_WIDTH, dtype=jnp.float32) / (MODEL_WIDTH - 1)
    lowest, highest = (0.5, 2.5)
    jitter = jnp.exp(jax.random.uniform(key, (MODEL_WIDTH,), jnp.float32, math.log(0.8), math.log(1.25)))
    return jnp.exp(math.log(lowest) + math.log(highest / lowest) * position) * jitter


def draw_gate_weight(key, part):
    first_key = jax.random.fold_in(key, 11)
    second_key = jax.random.fold_in(key, 23)
    scale = 1.0 / math.sqrt(MODEL_WIDTH)
    entries = jnp.clip(jax.random.normal(first_key, (MODEL_WIDTH, MODEL_WIDTH), jnp.float32), -4.0, 4.0)
    shared = jnp.clip(1.5 * jax.random.normal(second_key, (1, MODEL_WIDTH), jnp.float32), -3.75, 3.75)
    return (scale * (entries + shared)).astype(jnp.bfloat16)


def strengthened(values, own_key, source, target, shards_of, factor):
    owner, partner = [(jnp.arange(values.shape[dim]) // (values.shape[dim] // shards_of)).reshape([-1 if axis == dim else 1 for axis in range(values.ndim)]) for dim in (source, target)]
    chosen = jax.random.permutation(own_key, shards_of)[partner]
    strong = (owner == chosen) | (owner == (partner + shards_of // 2) % shards_of)
    return jnp.where(strong, factor * values, values)


def block_scale(key, dims, pieces, least, top_value):
    factor_of, own = 1.0, jax.random.fold_in(key, 6)
    for axis_at, blocks in pieces:
        steps = jnp.exp(jax.random.uniform(jax.random.fold_in(own, axis_at), (blocks,), jnp.float32, least / len(pieces), top_value / len(pieces)))
        factor_of = factor_of * jnp.repeat(steps, dims[axis_at] // blocks).reshape([-1 if axis == axis_at else 1 for axis in range(len(dims))])
    return factor_of


def scatter_about(rng, extent, spread, bound, pieces=(), kind=jnp.bfloat16):
    result = spread * jax.random.normal(rng, extent, jnp.float32)
    if pieces:
        result = result * block_scale(rng, extent, pieces, -0.22, 0.18)
    return jnp.clip(result, -bound, bound).astype(kind)


def bell_draw_with(own_key, shape, scale, limit, split, heavy, kind=jnp.bfloat16):
    values = scale * jax.random.normal(own_key, shape, jnp.float32)
    if split:
        values = values * block_scale(own_key, shape, split, -0.22, 0.18)
    return jnp.clip(strengthened(values, jax.random.fold_in(own_key, 3), *heavy), -limit, limit).astype(kind)


def setup_inputs(seed: int = 0, part: int = 0) -> dict:
    arg_keys = jax.random.split(jax.random.key(seed), 8)
    own_keys = jax.random.split(jax.random.fold_in(arg_keys[7], part), 8)
    features = scatter_about(own_keys[0], (UTT, FRAMES, MODEL_WIDTH), 1.0, 6.0, ((0, 2), (1, 2), (2, 4)))
    output_gradient = scatter_about(own_keys[1], (UTT, FRAMES, MODEL_WIDTH), 1.0, 6.0, ((0, 2), (1, 2), (2, 4)))
    value_weight = bell_draw_with(arg_keys[2], (MODEL_WIDTH, MODEL_WIDTH), MODEL_WIDTH ** -0.5, 0.109375, ((0, 2), (1, 4)), (1, 0, 4, 2.0))
    gate_weight = draw_gate_weight(jax.random.fold_in(arg_keys[7], 71), part)
    mixer_weight = bell_draw_with(arg_keys[4], (MODEL_WIDTH, MODEL_WIDTH), MODEL_WIDTH ** -0.5, 0.109375, ((0, 2), (1, 4)), (1, 0, 4, 2.0))
    conv_kernel = scatter_about(arg_keys[5], (KERNEL, MODEL_WIDTH), KERNEL ** -0.5, 1.0, ((1, 4),), jnp.float32)
    layer_norm_gain = draw_layer_norm_gain(jax.random.fold_in(arg_keys[7], 71), part)
    return dict(features=features, output_gradient=output_gradient, value_weight=value_weight, gate_weight=gate_weight, mixer_weight=mixer_weight, conv_kernel=conv_kernel, layer_norm_gain=layer_norm_gain)


EPS = 1e-05

def rounded(values):
    return lax.optimization_barrier(values.astype(jnp.bfloat16)).astype(jnp.float32)

def block_products(pairs, row_span):
    width = MODEL_WIDTH // N_COL
    contract_last = (((1,), (1,)), ((), ()))

    def add_block(block, total):
        start = jnp.asarray(block, jnp.int32) * width
        partial_value = jnp.zeros((row_span, MODEL_WIDTH), jnp.float32)
        for left, weights in pairs:
            left_cols = lax.dynamic_slice_in_dim(left, start, width, 1)
            weight_cols = lax.dynamic_slice_in_dim(weights, start, width, 1)
            partial_value = partial_value + lax.dot_general(left_cols, weight_cols, contract_last, preferred_element_type=jnp.float32)
        return total + rounded(partial_value)
    return lax.fori_loop(0, N_COL, add_block, jnp.zeros((row_span, MODEL_WIDTH), jnp.float32))

def weight_grad(left, right):
    total = jnp.zeros((left.shape[2], right.shape[2]), jnp.float32)
    for dp_index in range(N_DP):
        for row_index in range(N_ROW):
            left_block = left[dp_index * UTT_DEV:(dp_index + 1) * UTT_DEV, row_index * TF_DEV:(row_index + 1) * TF_DEV]
            right_block = right[dp_index * UTT_DEV:(dp_index + 1) * UTT_DEV, row_index * TF_DEV:(row_index + 1) * TF_DEV]
            partial_value = lax.dot_general(left_block.reshape(-1, left.shape[2]), right_block.reshape(-1, right.shape[2]), (((0,), (0,)), ((), ())), preferred_element_type=jnp.float32)
            total = total + rounded(partial_value)
    return total

def reference(features, output_gradient, value_weight, gate_weight, mixer_weight, conv_kernel, layer_norm_gain):
    row_span = UTT * FRAMES
    half = KERNEL // 2
    feat_float = features.astype(jnp.float32)
    row_average = lax.optimization_barrier(jnp.mean(feat_float, -1, keepdims=True))
    centered_input = feat_float - row_average
    variance = lax.optimization_barrier(jnp.mean(centered_input * centered_input, -1, keepdims=True))
    inverse_deviation = lax.rsqrt(variance + EPS)
    standardized_input = centered_input * inverse_deviation
    normalized_rows = (standardized_input * layer_norm_gain).astype(jnp.bfloat16)
    normed_rows = normalized_rows.reshape(row_span, MODEL_WIDTH)
    value = jnp.dot(normed_rows, value_weight, preferred_element_type=jnp.float32)
    gate = jnp.dot(normed_rows, gate_weight, preferred_element_type=jnp.float32)
    sig_gate = jax.nn.sigmoid(gate)
    glu = (value * sig_gate).astype(jnp.bfloat16).reshape(UTT, FRAMES, MODEL_WIDTH)
    glu_pad = jnp.pad(glu, ((0, 0), (half, half), (0, 0)))
    conv = jnp.zeros((UTT, FRAMES, MODEL_WIDTH), jnp.float32)
    for kernel_tap in range(KERNEL):
        conv = conv + conv_kernel[kernel_tap] * glu_pad[:, kernel_tap:kernel_tap + FRAMES].astype(jnp.float32)
    sig_conv = jax.nn.sigmoid(conv)
    mixed = (conv * sig_conv).astype(jnp.bfloat16)
    projected = jnp.dot(mixed.reshape(row_span, MODEL_WIDTH), mixer_weight, preferred_element_type=jnp.float32)
    module_out = (feat_float + projected.reshape(UTT, FRAMES, MODEL_WIDTH)).astype(jnp.bfloat16)
    grad_rows = output_gradient.reshape(row_span, MODEL_WIDTH)
    mixed_grad = block_products([(grad_rows, mixer_weight)], row_span).reshape(UTT, FRAMES, MODEL_WIDTH)
    swish_slope = sig_conv * (1.0 + conv * (1.0 - sig_conv))
    conv_grad = (mixed_grad * swish_slope).astype(jnp.bfloat16)
    grad_pad = jnp.pad(conv_grad, ((0, 0), (half, half), (0, 0)))
    glu_grad = jnp.zeros((UTT, FRAMES, MODEL_WIDTH), jnp.float32)
    kernel_rows = []
    for kernel_tap in range(KERNEL):
        back = 2 * half - kernel_tap
        glu_grad = glu_grad + conv_kernel[kernel_tap] * grad_pad[:, back:back + FRAMES].astype(jnp.float32)
        kernel_rows.append(lax.optimization_barrier(jnp.sum(glu_pad[:, kernel_tap:kernel_tap + FRAMES].astype(jnp.float32) * conv_grad.astype(jnp.float32), axis=(0, 1))))
    kernel_grad = jnp.stack(kernel_rows)
    glu_grad = glu_grad.reshape(row_span, MODEL_WIDTH)
    value_grad = (glu_grad * sig_gate).astype(jnp.bfloat16)
    gate_grad = (glu_grad * value * sig_gate * (1.0 - sig_gate)).astype(jnp.bfloat16)
    normalized_gradient = block_products([(value_grad, value_weight), (gate_grad, gate_weight)], row_span).reshape(UTT, FRAMES, MODEL_WIDTH)
    norm_gain_gradient = lax.optimization_barrier(jnp.sum(normalized_gradient * standardized_input, axis=(0, 1)))
    scaled_rows = normalized_gradient * layer_norm_gain
    gradient_mean = lax.optimization_barrier(jnp.mean(scaled_rows, -1, keepdims=True))
    projected_mean = lax.optimization_barrier(jnp.mean(scaled_rows * standardized_input, -1, keepdims=True))
    input_gradient = (output_gradient.astype(jnp.float32) + (scaled_rows - gradient_mean - standardized_input * projected_mean) * inverse_deviation).astype(jnp.bfloat16)
    value_weight_grad = weight_grad(normalized_rows, value_grad.reshape(UTT, FRAMES, MODEL_WIDTH))
    gate_weight_grad = weight_grad(normalized_rows, gate_grad.reshape(UTT, FRAMES, MODEL_WIDTH))
    mixer_weight_grad = weight_grad(mixed, output_gradient)
    return (module_out, input_gradient, value_weight_grad, gate_weight_grad, mixer_weight_grad, kernel_grad, norm_gain_gradient)
```

```python
import jax
import jax.numpy as jnp
from jax import lax
from jax.sharding import PartitionSpec as P

EPS = 1e-05
CONTRACT_LAST = (((1,), (1,)), ((), ()))
CONTRACT_FIRST = (((0,), (0,)), ((), ()))
BF16 = jnp.bfloat16
F32 = jnp.float32


def ring(count, shift):
    return [(i, (i + shift) % count) for i in range(count)]


def gather_over(x, axis):
    count, me = lax.axis_size(axis), lax.axis_index(axis)
    pieces = [x] + [lax.ppermute(x, axis, ring(count, s)) for s in range(1, count)]
    ordered = []
    for j in range(count):
        back = (me - j) % count
        block = pieces[0]
        for s in range(1, count):
            block = jnp.where(back == s, pieces[s], block)
        ordered.append(block)
    return ordered


def scatter_over(part, axis, dim, dtype):
    count, me = lax.axis_size(axis), lax.axis_index(axis)
    width = part.shape[dim] // count
    total = lax.dynamic_slice_in_dim(part, me * width, width, dim)
    for s in range(1, count):
        sent = lax.dynamic_slice_in_dim(part, ((me + s) % count) * width, width, dim)
        total = total + lax.ppermute(sent.astype(dtype), axis, ring(count, s)).astype(F32)
    return total


def spread_over(x, axis, dim):
    count, me = lax.axis_size(axis), lax.axis_index(axis)
    width = x.shape[dim] // count
    blocks = [lax.dynamic_slice_in_dim(x, me * width, width, dim)]
    for s in range(1, count):
        sent = lax.dynamic_slice_in_dim(x, ((me + s) % count) * width, width, dim)
        blocks.append(lax.ppermute(sent, axis, ring(count, s)))
    return jnp.concatenate(blocks, axis=0)


def collect_over(x, axis):
    count = lax.axis_size(axis)
    return jnp.concatenate(
        [x] + [lax.ppermute(x, axis, ring(count, s)) for s in range(1, count)], axis=0
    )


def shards(
    features, output_gradient, value_weight, gate_weight, mixer_weight, conv_kernel, layer_norm_gain
):
    utts, frames, width = features.shape
    taps = conv_kernel.shape[0]
    half = taps // 2
    model = layer_norm_gain.shape[0]
    n_row, n_col = lax.axis_size("row"), lax.axis_size("col")
    row, col = lax.axis_index("row"), lax.axis_index("col")
    per_row = n_col // n_row
    depth = per_row * width
    narrow = width // n_row
    span = n_row * frames
    cells = utts * span
    turned = [
        (r * n_col + h * per_row + i, h * n_col + r * per_row + i)
        for r in range(n_row)
        for h in range(n_row)
        for i in range(per_row)
    ]

    def turn(x):
        return lax.ppermute(x, ("row", "col"), turned)

    own = features.astype(F32)
    block_mean = jnp.mean(own, -1)
    block_square = jnp.sum((own - block_mean[..., None]) ** 2, -1)
    stats = lax.all_gather(jnp.stack([block_mean, block_square]), ("row", "col"), axis=0)
    stats = stats.reshape(n_row, n_col, 2, utts, frames)
    mean = jnp.mean(stats[:, :, 0], 1)
    square = jnp.sum(stats[:, :, 1] + width * (stats[:, :, 0] - mean[:, None]) ** 2, 1)
    inverse = lax.rsqrt(square / model + EPS)
    mean_own = lax.dynamic_index_in_dim(mean, row, 0, keepdims=False)[..., None]
    inverse_own = lax.dynamic_index_in_dim(inverse, row, 0, keepdims=False)[..., None]
    mean_all, inverse_all = (
        jnp.swapaxes(s, 0, 1)[:, :, :, None, None] for s in (mean, inverse)
    )

    inputs = lax.all_gather(turn(features), "col", axis=0)
    inputs = inputs.reshape(n_row, per_row, utts, frames, width).transpose(2, 0, 3, 1, 4)
    gain_rows = lax.dynamic_slice_in_dim(layer_norm_gain, row * depth, depth, 0)
    normed = (
        ((inputs.astype(F32) - mean_all) * inverse_all * gain_rows.reshape(per_row, width))
        .astype(BF16)
        .reshape(cells, depth)
    )
    gate_part = jnp.dot(normed, gate_weight, preferred_element_type=F32)
    gate = scatter_over(gate_part, "row", 1, GATE_DTYPE)
    value_part = jnp.dot(normed, value_weight, preferred_element_type=F32)
    value = scatter_over(value_part, "row", 1, BF16)

    grad_rows = jnp.stack(gather_over(output_gradient, "row"), axis=1).reshape(cells, width)
    mixed_part = lax.dot_general(
        grad_rows, mixer_weight, CONTRACT_LAST, preferred_element_type=F32
    ).astype(BF16)
    mixed_part = mixed_part.reshape(cells, per_row, n_row, narrow).transpose(2, 1, 0, 3)
    mixed_grad = turn(
        lax.psum_scatter(
            mixed_part.reshape(n_col * cells, narrow), "col", scatter_dimension=0, tiled=True
        )
    )
    mixed_grad = mixed_grad.astype(F32).reshape(utts, span, narrow)

    kernel_own = lax.dynamic_slice_in_dim(conv_kernel, row * narrow, narrow, 1)
    sig_gate = jax.nn.sigmoid(gate)
    glu = (value * sig_gate).astype(BF16).reshape(utts, span, narrow)
    glu_pad = jnp.pad(glu, ((0, 0), (half, half), (0, 0)))
    conv = jnp.zeros((utts, span, narrow), F32)
    for tap in range(taps):
        conv = conv + kernel_own[tap] * glu_pad[:, tap : tap + span].astype(F32)
    sig_conv = jax.nn.sigmoid(conv)
    mixed = (conv * sig_conv).astype(BF16)
    conv_grad = (mixed_grad * (sig_conv * (1.0 + conv * (1.0 - sig_conv)))).astype(BF16)

    grad_pad = jnp.pad(conv_grad, ((0, 0), (half, half), (0, 0)))
    conv_grad_float = conv_grad.astype(F32)
    glu_grad = jnp.zeros((utts, span, narrow), F32)
    kernel_rows = []
    for tap in range(taps):
        back = 2 * half - tap
        glu_grad = glu_grad + kernel_own[tap] * grad_pad[:, back : back + span].astype(F32)
        kernel_rows.append(
            jnp.sum(glu_pad[:, tap : tap + span].astype(F32) * conv_grad_float, axis=(0, 1))
        )
    glu_grad = glu_grad.reshape(cells, narrow)
    value_grad = (glu_grad * sig_gate).astype(BF16)
    gate_grad = (glu_grad * value * sig_gate * (1.0 - sig_gate)).astype(BF16)
    value_grad, gate_grad = (
        jnp.concatenate(gather_over(g, "row"), axis=1) for g in (value_grad, gate_grad)
    )

    normed_part = (
        lax.dot_general(value_grad, value_weight, CONTRACT_LAST, preferred_element_type=F32)
        + lax.dot_general(gate_grad, gate_weight, CONTRACT_LAST, preferred_element_type=F32)
    ).astype(BF16)
    normed_part = normed_part.reshape(utts, n_row, frames, per_row, width).transpose(1, 3, 0, 2, 4)
    normed_grad = turn(
        lax.psum_scatter(
            normed_part.reshape(n_col * utts * frames, width),
            "col",
            scatter_dimension=0,
            tiled=True,
        )
    )
    normed_grad = normed_grad.astype(F32).reshape(utts, frames, width)

    mixed_rows = lax.all_gather(turn(mixed), "col", axis=0)
    mixed_rows = (
        mixed_rows.reshape(n_row, per_row, utts, span, narrow)
        .transpose(2, 3, 1, 0, 4)
        .reshape(cells, depth)
    )
    projected = jnp.dot(mixed_rows, mixer_weight, preferred_element_type=F32)
    projected = scatter_over(projected.reshape(utts, span, width), "row", 1, BF16)
    module_out = (own + projected).astype(BF16)

    normed_cells = spread_over(normed, "dp", 1)
    value_weight_grad, gate_weight_grad = (
        lax.dot_general(
            normed_cells, collect_over(g, "dp"), CONTRACT_FIRST, preferred_element_type=F32
        )
        for g in (value_grad, gate_grad)
    )
    mixer_weight_grad = lax.dot_general(
        spread_over(mixed_rows, "dp", 1),
        collect_over(grad_rows, "dp"),
        CONTRACT_FIRST,
        preferred_element_type=F32,
    )
    kernel_parts = lax.all_gather(jnp.stack(kernel_rows), ("row", "dp"), axis=0)
    kernel_parts = kernel_parts.reshape(n_row, -1, taps, narrow)
    kernel_grad = jnp.sum(kernel_parts, 1).transpose(1, 0, 2).reshape(taps, width)

    standardized = (own - mean_own) * inverse_own
    gain_own = lax.dynamic_slice_in_dim(layer_norm_gain, col * width, width, 0)
    scaled = normed_grad * gain_own
    sums = lax.psum(jnp.stack([jnp.sum(scaled, -1), jnp.sum(scaled * standardized, -1)]), "col")
    input_gradient = (
        output_gradient.astype(F32)
        + (scaled - sums[0][..., None] / model - standardized * (sums[1][..., None] / model))
        * inverse_own
    ).astype(BF16)
    norm_gain_gradient = lax.psum(jnp.sum(normed_grad * standardized, axis=(0, 1)), ("row", "dp"))
    return (
        module_out,
        input_gradient,
        value_weight_grad,
        gate_weight_grad,
        mixer_weight_grad,
        kernel_grad,
        norm_gain_gradient,
    )


GATE_DTYPE = F32


def solution(mesh):
    placed = (
        P(("groups", "dp"), "row", "col"),
        P(("groups", "dp"), "row", "col"),
        P("row", "col"),
        P("row", "col"),
        P("row", "col"),
        P(None, "col"),
        P(),
    )
    return jax.shard_map(
        shards,
        mesh=mesh,
        in_specs=placed,
        out_specs=(
            P(("groups", "dp"), "row", "col"),
            P(("groups", "dp"), "row", "col"),
            P(("groups", "row", "dp"), "col"),
            P(("groups", "row", "dp"), "col"),
            P(("groups", "row", "dp"), "col"),
            P("groups", "col"),
            P(("groups", "col")),
        ),
        check_vma=False,
    )
```
